32 devices in a mesh: grp: 2 (over x), tm: 8 (over z, y), head: 2 (over core).
Axes of the slice: x: 2, y: 2, z: 4, core: 2. Of those that a mesh axis runs over, the one named last changes fastest.
Arguments:
- queries: bfloat16 [2048, 6144], P(('grp', 'tm'), 'head'), parts along dimension 0, may hold values from -130 to 130
- keys: bfloat16 [2048, 1024], P(('grp', 'tm'), 'head'), parts along dimension 0, may hold values from -7 to 7
- values: bfloat16 [2048, 1024], P(('grp', 'tm'), 'head'), parts along dimension 0, may hold values from -6 to 6
- span_mask: int32 [8, 4], P('grp'), parts along dimension 0, may hold values from 0 to 1, as said below
- section: int32 [8], P('grp'), parts along dimension 0, may hold values from 0 to 3
- section_gate: float32 [4, 6144], P(None, 'head'), may hold values from 0.1 to 1.9
Outputs:
- mixed: bfloat16 [2048, 6144], P(('grp', 'tm'), 'head'), parts along dimension 0
- log_total: float32 [48, 2048], P('head', ('grp', 'tm')), parts along dimension 1
The draws below stay inside these ranges and needn't reach their ends.
There are 2 independent parts, one for each index of `grp`. The reference program is written for one: setup_inputs(seed, part) draws one part's arguments, and reference() takes and returns one part's arrays. A program takes and returns all parts, laid end to end along the dimension named above; an argument that names none is the same for every part. Nothing has to cross between parts.
Inputs may be any that keep to these rules, and one draw needn't show every extreme that they name: `span_mask`: the first column and the diagonal are 1 and everything above the diagonal is 0.
All inputs are finite; a program needn't handle non-finite values.
Results may differ from the reference program's by a relative error of at most 0.006.
Values may be sent and summed in bfloat16 or wider, within the bound.
A program may use at most 64 MiB of HBM per device.

```python
import math
import jax
import jax.numpy as jnp
from jax import lax

QUERY_HEADS = 48
KEY_VALUE_HEADS = 8
HEAD_SIZE = 128
CH = 256
SECTIONS = 4
CLIP_TOKENS = 1024
NC = 4


def paired_fields(key):
    base = jax.random.fold_in(key, 7)
    random_key_first, key_b = jax.random.split(base, 2)
    keys_float = jnp.clip(jax.random.normal(random_key_first, (CLIP_TOKENS, KEY_VALUE_HEADS * HEAD_SIZE), jnp.float32), -6.0, 6.0)
    queries_f = 2.0 * jnp.clip(jax.random.normal(key_b, (CLIP_TOKENS, QUERY_HEADS * HEAD_SIZE), jnp.float32), -6.0, 6.0)
    return (queries_f, keys_float)


def draw_queries(key, part):
    return paired_fields(key)[0].astype(jnp.bfloat16)


def draw_keys(key, part):
    return paired_fields(key)[1].astype(jnp.bfloat16)


def draw_span_mask(key, part):
    coin = jax.random.randint(jax.random.fold_in(key, 11), (NC, NC), 0, 2)
    row_ids = jnp.arange(NC, dtype=jnp.int32)[:, None]
    col_ids = jnp.arange(NC, dtype=jnp.int32)[None, :]
    result = jnp.where(col_ids < row_ids, coin, 0)
    result = jnp.where(col_ids == row_ids, 1, result)
    result = jnp.where(col_ids == 0, 1, result)
    return result.astype(jnp.int32)


def touch_ends(drawn, stream_key, low, largest):
    dims = drawn.shape
    place = [jax.random.randint(jax.random.fold_in(stream_key, axis), (), 0, dims[axis]) for axis in range(len(dims))]
    drawn = drawn.at[tuple(place)].set(low)
    longest = dims.index(max(dims))
    place[longest] = (place[longest] + 1) % dims[longest]
    return drawn.at[tuple(place)].set(largest)


def block_scale(own_key, shape, shards, least, high):
    factor_of, own = 1.0, jax.random.fold_in(own_key, 6)
    for axis_at, parts in shards:
        heights = jnp.exp(jax.random.uniform(jax.random.fold_in(own, axis_at), (parts,), jnp.float32, least / len(shards), high / len(shards)))
        factor_of = factor_of * jnp.repeat(heights, shape[axis_at] // parts).reshape([-1 if axis == axis_at else 1 for axis in range(len(shape))])
    return factor_of


def scatter_about(stream_key, dims, deviation, most, shards=(), held_as=jnp.bfloat16):
    entries = deviation * jax.random.normal(stream_key, dims, jnp.float32)
    if shards:
        entries = entries * block_scale(stream_key, dims, shards, -0.22, 0.18)
    return jnp.clip(entries, -most, most).astype(held_as)


def setup_inputs(seed: int = 0, part: int = 0) -> dict:
    arg_keys = jax.random.split(jax.random.key(seed), 7)
    own_keys = jax.random.split(jax.random.fold_in(arg_keys[6], part), 7)
    queries = draw_queries(jax.random.fold_in(jax.random.fold_in(arg_keys[6], part), 71), part)
    keys = draw_keys(jax.random.fold_in(jax.random.fold_in(arg_keys[6], part), 71), part)
    values = scatter_about(own_keys[2], (CLIP_TOKENS, KEY_VALUE_HEADS * HEAD_SIZE), 1.0, 6.0, ((0, 8), (1, 2)))
    span_mask = draw_span_mask(jax.random.fold_in(jax.random.fold_in(arg_keys[6], part), 71), part)
    section = touch_ends(jax.random.randint(own_keys[4], (NC,), 0, SECTIONS), jax.random.fold_in(own_keys[4], 1), 0, SECTIONS - 1).astype(jnp.int32)
    section_gate = jnp.clip(1.0 + 0.18 * jax.random.normal(arg_keys[5], (SECTIONS, QUERY_HEADS * HEAD_SIZE), jnp.float32), 0.1, 1.9)
    return dict(queries=queries, keys=keys, values=values, span_mask=span_mask, section=section, section_gate=section_gate)


def reference(queries, keys, values, span_mask, section, section_gate):
    total_rows = queries.shape[0]
    query_group = QUERY_HEADS // KEY_VALUE_HEADS
    span_ids = (jnp.arange(total_rows, dtype=jnp.int32) // CH).astype(jnp.int32)
    allowed = jnp.take(jnp.take(span_mask, span_ids, axis=0), span_ids, axis=1) > 0
    scale = 1.0 / math.sqrt(HEAD_SIZE)

    def one_head(head_index):
        start_q = (head_index * HEAD_SIZE).astype(jnp.int32)
        start_k = (head_index // query_group * HEAD_SIZE).astype(jnp.int32)
        query_head = lax.dynamic_slice_in_dim(queries, start_q, HEAD_SIZE, 1)
        key_head = lax.dynamic_slice_in_dim(keys, start_k, HEAD_SIZE, 1)
        value_head = lax.dynamic_slice_in_dim(values, start_k, HEAD_SIZE, 1)
        score = jnp.dot(query_head, key_head.T, preferred_element_type=jnp.float32) * scale
        score = jnp.where(allowed, score, -1e+30)
        top = lax.optimization_barrier(jnp.max(score, axis=1))
        weight = jnp.where(allowed, jnp.exp(score - top[:, None]), 0.0)
        total = lax.optimization_barrier(jnp.sum(weight, axis=1))
        attended = jnp.dot(weight.astype(jnp.bfloat16), value_head, preferred_element_type=jnp.float32) / total[:, None]
        return (attended, top + jnp.log(total))
    attended, log_total = lax.map(one_head, jnp.arange(QUERY_HEADS, dtype=jnp.int32))
    attended = jnp.transpose(attended, (1, 0, 2)).reshape(total_rows, QUERY_HEADS * HEAD_SIZE)
    gate_rows = jnp.take(section_gate, jnp.take(section, span_ids), axis=0)
    mixed = (gate_rows * attended).astype(jnp.bfloat16)
    return (mixed, log_total)
```

```python
import functools
import math

import jax
import jax.numpy as jnp
from jax import lax
from jax.experimental import pallas as pl
from jax.experimental.pallas import tpu as pltpu
from jax.sharding import PartitionSpec as P

HEAD_SIZE = 128
CH = 256
MESH = pl.DeviceIdType.MESH
LOG2E = 1.4426950408889634
LN2 = 0.6931471805599453
FAR = 1e30


def kernel(
    pairs, far_from, q_hbm, k_hbm, v_hbm, mask_hbm, sec_hbm, gate_hbm, out_ref, lt_ref,
    qbuf, kv, top_s, tot_s, acc_s, ltm_s, gate_s, mask_ref, sec_ref, gate_ref,
    lent_out, lent_lt, lent_gate, home_lt,
    local_sem, recv_sem, up_sem, over_sem, lend_sem, back_sem,
):
    rows = qbuf.shape[1]
    kv_heads = kv.shape[1]
    group = lent_out.shape[0]
    q_heads = kv_heads * group
    tall = group * rows
    final = pairs - 1
    top_head = kv_heads - 1
    factor = LOG2E / math.sqrt(HEAD_SIZE)

    me = lax.axis_index("tm")
    pair = me // 2
    side = me % 2
    other = 1 - side
    partner = me + 1 - 2 * side
    has_prev = pair > 0
    has_next = pair < final
    at_bottom = pair == 0
    at_lender = pair == final
    at_helper = pair == final - 1
    at_middle = has_prev & (pair < final - 1)

    barrier = pltpu.get_barrier_semaphore()
    pl.semaphore_signal(barrier, inc=1, device_id={"tm": partner}, device_id_type=MESH)

    @pl.when(has_next)
    def _():
        pl.semaphore_signal(barrier, inc=1, device_id={"tm": me + 2}, device_id_type=MESH)

    @pl.when(has_prev)
    def _():
        pl.semaphore_signal(barrier, inc=1, device_id={"tm": me - 2}, device_id_type=MESH)

    pl.semaphore_wait(
        barrier, 1 + has_next.astype(jnp.int32) + has_prev.astype(jnp.int32)
    )

    def copy_to(source, target_ref, send, receive, target):
        return pltpu.make_async_remote_copy(
            src_ref=source,
            dst_ref=target_ref,
            send_sem=send,
            recv_sem=receive,
            device_id={"tm": target},
            device_id_type=MESH,
        )

    def columns(ref, h):
        return ref.at[:, pl.ds(h * HEAD_SIZE, HEAD_SIZE)]

    def unit(span, edge, h):
        return kv.at[span, h, :, edge]

    def own(send, target, h):
        for i, source in enumerate((k_hbm, v_hbm)):
            copy_to(
                columns(source, h), kv.at[pair, h, i, side],
                send.at[pair], recv_sem.at[me, h], target,
            ).start()

    def own_up(h):
        own(up_sem, me + 2, h)

    def own_over(h):
        own(over_sem, partner, h)

    def move(span, edge, h, send, target):
        piece = unit(span, edge, h)
        return copy_to(piece, piece, send, recv_sem.at[2 * span + edge, h], target)

    def arrive(span, edge, h):
        move(span, edge, h, over_sem.at[span], partner).wait_recv()

    def up(span, h):
        move(span, side, h, up_sem.at[span], me + 2).start()

    def over(span, h):
        if isinstance(h, int) and h < far_from:
            move(span, side, h, over_sem.at[span], partner).start()
        else:

            @pl.when((span > 0) | (h < far_from))
            def _():
                move(span, side, h, over_sem.at[span], partner).start()

    def far_up(h):
        return move(0, other, h, up_sem.at[pairs], me + 2)

    def sent(sem, low, high):
        some = kv.at[0, pl.ds(low, high - low), :, 0]
        copy_to(some, some, sem, recv_sem.at[0, 0], partner).wait_send()

    def lend_q(j):
        return copy_to(columns(q_hbm, j), qbuf.at[q_heads + j], lend_sem.at[0], lend_sem.at[1], me - 2)

    def lent_q():
        whole = qbuf.at[pl.ds(q_heads, group)]
        return copy_to(whole, whole, lend_sem.at[0], lend_sem.at[1], me - 2)

    def give_back(j):
        return copy_to(lent_out.at[j], columns(out_ref, j), back_sem.at[0], back_sem.at[1], me + 2)

    def given():
        return copy_to(lent_out, lent_out, back_sem.at[0], back_sem.at[1], me + 2)

    def give_totals():
        return copy_to(lent_lt, home_lt, back_sem.at[2], back_sem.at[3], me + 2)

    heads = range(kv_heads)

    @pl.when(at_bottom)
    def _():
        for h in heads:
            own_up(h)
            own_over(h)

    @pl.when(at_middle)
    def _():
        for h in heads:
            if h < top_head:
                own_up(h)
            own_over(h)

    @pl.when(at_helper)
    def _():
        for h in heads:
            if h > 0:
                own_up(h)
            if h < 2:
                own_over(h)

    @pl.when(at_lender)
    def _():
        own(up_sem, me - 2, 0)
        for h in heads:
            if h > 0:
                own_over(h)
        for j in range(group):
            lend_q(j).start()

    small = [
        pltpu.make_async_copy(mask_hbm, mask_ref, local_sem.at[0]),
        pltpu.make_async_copy(sec_hbm, sec_ref, local_sem.at[1]),
        pltpu.make_async_copy(gate_hbm, gate_ref, local_sem.at[2]),
    ]
    for copy in small:
        copy.start()
    for h in heads:
        for i, source in enumerate((k_hbm, v_hbm)):
            pltpu.make_async_copy(columns(source, h), kv.at[pair, h, i, side], local_sem.at[3]).start()
    for h in range(q_heads):
        pltpu.make_async_copy(columns(q_hbm, h), qbuf.at[h], local_sem.at[4]).start()
    for copy in small:
        copy.wait()
    mine = kv.at[pair, :, :, side]
    pltpu.make_async_copy(mine, mine, local_sem.at[3]).wait()
    mine = qbuf.at[pl.ds(0, q_heads)]
    pltpu.make_async_copy(mine, mine, local_sem.at[4]).wait()

    def gate_of(span, width):
        row = gate_ref[pl.ds(0, 1), :width]
        for i in range(1, gate_ref.shape[0]):
            row = jnp.where(sec_ref[span] == i, gate_ref[pl.ds(i, 1), :width], row)
        return row

    gate_s[...] = gate_of(pair, gate_s.shape[1])
    lent_gate[...] = gate_of(final, lent_gate.shape[1])
    ltm_s[...] = jnp.zeros_like(ltm_s)

    def visit(span, head, first, last, lent=False):
        base = q_heads if lent else head * group
        ok = mask_ref[final if lent else pair, span] > 0
        keys = kv[span, head, 0].reshape(2 * rows, HEAD_SIZE)
        vals = kv[span, head, 1].reshape(2 * rows, HEAD_SIZE)

        def held(ref):
            return ref[pl.ds(base, group)].reshape(tall, HEAD_SIZE)

        def keep(ref, value):
            ref[pl.ds(base, group)] = value.reshape(group, rows, HEAD_SIZE)

        score = factor * lax.dot_general(
            held(qbuf), keys, (((1,), (1,)), ((), ())),
            preferred_element_type=jnp.float32,
        )
        top = jnp.where(ok, jnp.max(score, axis=1, keepdims=True), -FAR)
        if not first:
            before = held(top_s)
            top = jnp.maximum(before, top)
        top = jnp.broadcast_to(top, (tall, HEAD_SIZE))
        less = jnp.where(ok, top, FAR)
        weights = [
            jnp.exp2(score[:, i:i + HEAD_SIZE] - less)
            for i in range(0, score.shape[1], HEAD_SIZE)
        ]
        total = functools.reduce(jnp.add, weights)
        weight = jnp.concatenate([w.astype(jnp.bfloat16) for w in weights], axis=1)
        acc = jnp.dot(weight, vals, preferred_element_type=jnp.float32)
        if not first:
            fade = jnp.exp2(before - top)
            total = total + held(tot_s) * fade
            acc = acc + held(acc_s) * fade
        if not last:
            keep(top_s, top)
            keep(tot_s, total)
            keep(acc_s, acc)
            return
        lane = lax.broadcasted_iota(jnp.int32, (rows, HEAD_SIZE), 1)
        sums = jnp.zeros_like(ltm_s) if lent else ltm_s[...]
        full = jnp.sum(total, axis=1, keepdims=True)
        attended = acc / full
        log_total = top * LN2 + jnp.log(full)
        for t in range(group):
            cut = slice(t * rows, (t + 1) * rows)
            if lent:
                cols = slice(t * HEAD_SIZE, (t + 1) * HEAD_SIZE)
                lent_out[t] = (lent_gate[:, cols] * attended[cut]).astype(lent_out.dtype)
                sums = jnp.where(lane == t, log_total[cut], sums)
            else:
                j = base + t
                cols = pl.ds(pl.multiple_of(j * HEAD_SIZE, HEAD_SIZE), HEAD_SIZE)
                out_ref[:, cols] = (gate_s[:, cols] * attended[cut]).astype(out_ref.dtype)
                sums = jnp.where(lane == j, log_total[cut], sums)
        if lent:
            lent_lt[...] = jnp.transpose(sums)[:lent_lt.shape[0]]
        else:
            ltm_s[...] = sums

    def loop(low, high, body):
        def step(i, carry):
            body(i)
            return carry

        lax.fori_loop(low, high, step, 0)

    @pl.when(at_bottom)
    def _():
        for h in range(far_from, kv_heads):
            arrive(pair, other, h)
            far_up(h).start()

        def all_heads(h):
            @pl.when(h < far_from)
            def _():
                arrive(pair, other, h)

            visit(pair, h, True, True)

        loop(0, kv_heads, all_heads)
        sent(up_sem.at[0], 0, kv_heads)
        sent(over_sem.at[0], 0, kv_heads)
        sent(up_sem.at[pairs], far_from, kv_heads)

    @pl.when(at_middle)
    def _():
        def pass_on(i):
            span = pair - i
            for h in heads:
                arrive(span, side, h)
                up(span, h)
                over(span, h)
                if h == 0:

                    @pl.when(i == 1)
                    def _():
                        own_up(top_head)

            @pl.when(span == 0)
            def _():
                for h in range(far_from, kv_heads):
                    arrive(0, other, h)
                    far_up(h).start()

        pass_on(1)

        def own_span(h):
            arrive(pair, other, h)
            visit(pair, h, True, False)

        loop(0, kv_heads, own_span)

        def further(i):
            pass_on(i)

            def between(h):
                arrive(pair - i + 1, other, h)
                visit(pair - i + 1, h, False, False)

            loop(0, kv_heads, between)

        loop(2, pair + 1, further)

        def ending(h):
            @pl.when(h < far_from)
            def _():
                arrive(0, other, h)

            visit(0, h, False, True)

        loop(0, kv_heads, ending)

        def settle(span):
            sent(up_sem.at[span], 0, kv_heads)
            sent(over_sem.at[span], 0, kv_heads)

        loop(1, pair + 1, settle)
        sent(up_sem.at[0], 0, kv_heads)
        sent(over_sem.at[0], 0, far_from)
        sent(up_sem.at[pairs], far_from, kv_heads)

    @pl.when(at_helper)
    def _():
        arrive(pair - 1, side, 0)
        over(pair - 1, 0)
        arrive(final, side, 0)
        over(final, 0)
        for h in heads:
            if h >= 2:
                own_over(h)
        for h in range(1, top_head):
            arrive(pair - 1, side, h)
            up(pair - 1, h)
        arrive(pair, other, 0)
        visit(pair, 0, True, False)
        lent_q().wait_recv()
        visit(pair, 0, True, False, lent=True)
        arrive(final, other, 0)
        visit(final, 0, False, False, lent=True)

        def further(i):
            span = pair - i
            arrive(span, side, 0)
            over(span, 0)
            for h in range(1, top_head):
                over(span + 1, h)
            arrive(span + 1, side, top_head)
            up(span + 1, top_head)
            over(span + 1, top_head)
            arrive(span + 1, other, 0)
            visit(span + 1, 0, False, False, lent=True)

            def own_span(h):
                @pl.when(i == 2)
                def _():
                    arrive(pair, other, h)
                    visit(pair, h, True, False)

            own_span(1)

            def rest(h):
                arrive(span, side, h)
                up(span, h)
                own_span(h + 1)

            loop(1, top_head, rest)

        loop(2, pair + 1, further)
        for h in range(1, top_head):
            over(0, h)
        arrive(0, other, 0)
        visit(0, 0, False, True, lent=True)
        arrive(0, side, top_head)
        up(0, top_head)
        over(0, top_head)
        for j in range(group):
            give_back(j).start()
        give_totals().start()

        def remaining(i, last):
            span = pair - i

            def all_heads(h):
                @pl.when(h > 0)
                def _():
                    arrive(span, other, h)

                visit(span, h, False, last)

            loop(0, kv_heads, all_heads)

        loop(1, pair, lambda i: remaining(i, False))
        remaining(pair, True)

        def settle(span):
            sent(up_sem.at[span], 1, kv_heads)
            sent(over_sem.at[span], 0, kv_heads)

        loop(1, pair + 1, settle)
        sent(up_sem.at[0], 1, kv_heads)
        sent(over_sem.at[0], 0, far_from)
        sent(over_sem.at[final], 0, 1)
        given().wait_send()
        give_totals().wait_send()

    @pl.when(at_lender)
    def _():
        wide = kv_heads - 1

        def pass_on(n):
            span, h = pair - 1 - n // wide, 1 + n % wide
            arrive(span, side, h)
            move(span, side, h, over_sem.at[span], partner).start()

        def take(n, first, last):
            span, h = pair - n // wide, 1 + n % wide
            arrive(span, other, h)
            visit(span, h, first, last)

        def opening(n):
            pass_on(n)
            take(n, True, False)

        def between(n):
            pass_on(n)
            take(n, False, False)

        loop(0, wide, opening)
        loop(wide, wide * pair, between)
        loop(wide * pair, wide * (pair + 1), lambda n: take(n, False, True))

        sent(up_sem.at[pair], 0, 1)
        lent_q().wait_send()
        loop(0, pair + 1, lambda span: sent(over_sem.at[span], 1, kv_heads))
        given().wait_recv()
        give_totals().wait_recv()

    lt_ref[...] = jnp.transpose(ltm_s[...])[:q_heads]

    @pl.when(at_lender)
    def _():
        high = home_lt.shape[0]
        lt_ref[:high] = lt_ref[:high] + home_lt[...]


def finish(mixed_ref, log_ref, mixed_out, log_out, sem):
    parts = sem.shape[0] - 1
    high = mixed_ref.shape[0] // parts
    copies = [
        pltpu.make_async_copy(
            mixed_ref.at[pl.ds(i * high, high)],
            mixed_out.at[pl.ds(i * high, high)],
            sem.at[i],
        )
        for i in range(parts)
    ] + [pltpu.make_async_copy(log_ref, log_out, sem.at[parts])]
    for copy in copies:
        copy.start()
    for copy in copies:
        copy.wait()


def solution(mesh):
    count = mesh.shape["tm"]

    def on_device(queries, keys, values, span_mask, section, section_gate):
        rows = queries.shape[0]
        q_heads = queries.shape[1] // HEAD_SIZE
        kv_heads = keys.shape[1] // HEAD_SIZE
        group = q_heads // kv_heads
        assert CH == 2 * rows and count % 2 == 0 and count >= 8 and kv_heads > 2
        pairs = count // 2
        vmem = pl.BlockSpec(memory_space=pltpu.VMEM)
        dma = pltpu.SemaphoreType.DMA
        keep_near = lambda x: pltpu.with_memory_space_constraint(x, pltpu.VMEM)
        state = pltpu.VMEM((q_heads + group, rows, HEAD_SIZE), jnp.float32)
        held = pltpu.VMEM((pairs, kv_heads, 2, 2, rows, HEAD_SIZE), jnp.bfloat16)
        lent_lt = pltpu.VMEM((-(-group // 8) * 8, rows), jnp.float32)
        mixed, log_total = pl.pallas_call(
            functools.partial(kernel, pairs, kv_heads - 1),
            out_shape=(
                pltpu.VMEM(queries.shape, jnp.bfloat16),
                pltpu.VMEM((q_heads, rows), jnp.float32),
            ),
            in_specs=[pl.BlockSpec(memory_space=pltpu.HBM)] * 6,
            out_specs=(vmem, vmem),
            scratch_shapes=[
                pltpu.VMEM((q_heads + group, rows, HEAD_SIZE), jnp.bfloat16),
                held, state, state, state,
                pltpu.VMEM((rows, HEAD_SIZE), jnp.float32),
                pltpu.VMEM((1, queries.shape[1]), jnp.float32),
                pltpu.SMEM(span_mask.shape, jnp.int32),
                pltpu.SMEM(section.shape, jnp.int32),
                pltpu.VMEM(section_gate.shape, jnp.float32),
                pltpu.VMEM((group, rows, HEAD_SIZE), jnp.bfloat16),
                lent_lt,
                pltpu.VMEM((1, group * HEAD_SIZE), jnp.float32),
                lent_lt,
                dma((5,)), dma((count, kv_heads)), dma((pairs + 1,)), dma((pairs,)),
                dma((2,)), dma((4,)),
            ],
            compiler_params=pltpu.CompilerParams(
                collective_id=0, has_side_effects=True, vmem_limit_bytes=60*2**20
            ),
            name="span_attention",
        )(queries, keys, values, span_mask, section, section_gate)
        return pl.pallas_call(
            finish,
            out_shape=(
                jax.ShapeDtypeStruct(mixed.shape, mixed.dtype),
                jax.ShapeDtypeStruct(log_total.shape, log_total.dtype),
            ),
            in_specs=[vmem, vmem],
            out_specs=[pl.BlockSpec(memory_space=pltpu.HBM)] * 2,
            scratch_shapes=[dma((5,))],
            compiler_params=pltpu.CompilerParams(vmem_limit_bytes=4 * 2**20),
            name="write_back",
        )(keep_near(mixed), keep_near(log_total))

    placed = (
        P(("grp", "tm"), "head"),
        P(("grp", "tm"), "head"),
        P(("grp", "tm"), "head"),
        P("grp", None),
        P("grp"),
        P(None, "head"),
    )
    return jax.shard_map(
        on_device,
        mesh=mesh,
        in_specs=placed,
        out_specs=(P(("grp", "tm"), "head"), P("head", ("grp", "tm"))),
        check_vma=False,
    )
```

```python
import functools
import math

import jax
import jax.numpy as jnp
from jax import lax
from jax.experimental import pallas as pl
from jax.experimental.pallas import tpu as pltpu
from jax.sharding import PartitionSpec as P

HEAD_SIZE = 128
CH = 256
MESH = pl.DeviceIdType.MESH
LOG2E = 1.4426950408889634
LN2 = 0.6931471805599453
FAR = 1e30


def kernel(
    pairs, far_from, q_hbm, k_hbm, v_hbm, mask_hbm, sec_hbm, gate_hbm, out_ref, lt_ref,
    qbuf, kv, top_s, tot_s, acc_s, ltm_s, gate_s, mask_ref, sec_ref, gate_ref,
    lent_out, lent_lt, lent_gate, home_lt,
    local_sem, recv_sem, up_sem, over_sem, lend_sem, back_sem,
):
    rows = qbuf.shape[1]
    kv_heads = kv.shape[1]
    group = lent_out.shape[0]
    q_heads = kv_heads * group
    tall = group * rows
    final = pairs - 1
    top_head = kv_heads - 1
    factor = LOG2E / math.sqrt(HEAD_SIZE)

    me = lax.axis_index("tm")
    pair = me // 2
    side = me % 2
    other = 1 - side
    partner = me + 1 - 2 * side
    has_prev = pair > 0
    has_next = pair < final
    at_bottom = pair == 0
    at_lender = pair == final
    at_helper = pair == final - 1
    at_middle = has_prev & (pair < final - 1)

    barrier = pltpu.get_barrier_semaphore()
    pl.semaphore_signal(barrier, inc=1, device_id={"tm": partner}, device_id_type=MESH)

    @pl.when(has_next)
    def _():
        pl.semaphore_signal(barrier, inc=1, device_id={"tm": me + 2}, device_id_type=MESH)

    @pl.when(has_prev)
    def _():
        pl.semaphore_signal(barrier, inc=1, device_id={"tm": me - 2}, device_id_type=MESH)

    pl.semaphore_wait(
        barrier, 1 + has_next.astype(jnp.int32) + has_prev.astype(jnp.int32)
    )

    def copy_to(source, target_ref, send, receive, target):
        return pltpu.make_async_remote_copy(
            src_ref=source,
            dst_ref=target_ref,
            send_sem=send,
            recv_sem=receive,
            device_id={"tm": target},
            device_id_type=MESH,
        )

    def columns(ref, h):
        return ref.at[:, pl.ds(h * HEAD_SIZE, HEAD_SIZE)]

    def unit(span, edge, h):
        return kv.at[span, h, edge]

    def own(send, target, h):
        for i, source in enumerate((k_hbm, v_hbm)):
            copy_to(
                columns(source, h), kv.at[pair, h, side, i],
                send.at[pair], recv_sem.at[me, h], target,
            ).start()

    def own_up(h):
        own(up_sem, me + 2, h)

    def own_over(h):
        own(over_sem, partner, h)

    def move(span, edge, h, send, target):
        piece = unit(span, edge, h)
        return copy_to(piece, piece, send, recv_sem.at[2 * span + edge, h], target)

    def arrive(span, edge, h):
        move(span, edge, h, over_sem.at[span], partner).wait_recv()

    def up(span, h):
        move(span, side, h, up_sem.at[span], me + 2).start()

    def over(span, h):
        if isinstance(h, int) and h < far_from:
            move(span, side, h, over_sem.at[span], partner).start()
        else:

            @pl.when((span > 0) | (h < far_from))
            def _():
                move(span, side, h, over_sem.at[span], partner).start()

    def far_up(h):
        return move(0, other, h, up_sem.at[pairs], me + 2)

    def sent(sem, low, high):
        some = kv.at[0, pl.ds(low, high - low), 0]
        copy_to(some, some, sem, recv_sem.at[0, 0], partner).wait_send()

    def lend_q(j):
        return copy_to(columns(q_hbm, j), qbuf.at[q_heads + j], lend_sem.at[0], lend_sem.at[1], me - 2)

    def lent_q():
        whole = qbuf.at[pl.ds(q_heads, group)]
        return copy_to(whole, whole, lend_sem.at[0], lend_sem.at[1], me - 2)

    def give_back(j):
        return copy_to(lent_out.at[j], columns(out_ref, j), back_sem.at[0], back_sem.at[1], me + 2)

    def given():
        return copy_to(lent_out, lent_out, back_sem.at[0], back_sem.at[1], me + 2)

    def give_totals():
        return copy_to(lent_lt, home_lt, back_sem.at[2], back_sem.at[3], me + 2)

    heads = range(kv_heads)

    @pl.when(at_bottom)
    def _():
        for h in heads:
            own_up(h)
            own_over(h)

    @pl.when(at_middle)
    def _():
        for h in heads:
            if h > 0:
                own_up(h)
            own_over(h)

    @pl.when(at_helper)
    def _():
        for h in heads:
            if h > 0:
                own_up(h)
            if h < 2:
                own_over(h)

    @pl.when(at_lender)
    def _():
        own(up_sem, me - 2, 0)
        for h in heads:
            if h > 0:
                own_over(h)
        for j in range(group):
            lend_q(j).start()

    small = [
        pltpu.make_async_copy(mask_hbm, mask_ref, local_sem.at[0]),
        pltpu.make_async_copy(sec_hbm, sec_ref, local_sem.at[1]),
        pltpu.make_async_copy(gate_hbm, gate_ref, local_sem.at[2]),
    ]
    for copy in small:
        copy.start()
    for h in heads:
        for i, source in enumerate((k_hbm, v_hbm)):
            pltpu.make_async_copy(columns(source, h), kv.at[pair, h, side, i], local_sem.at[3]).start()
    for h in range(q_heads):
        pltpu.make_async_copy(columns(q_hbm, h), qbuf.at[h], local_sem.at[4]).start()
    for copy in small:
        copy.wait()
    mine = kv.at[pair, :, side]
    pltpu.make_async_copy(mine, mine, local_sem.at[3]).wait()
    mine = qbuf.at[pl.ds(0, q_heads)]
    pltpu.make_async_copy(mine, mine, local_sem.at[4]).wait()

    def gate_of(span, width):
        row = gate_ref[pl.ds(0, 1), :width]
        for i in range(1, gate_ref.shape[0]):
            row = jnp.where(sec_ref[span] == i, gate_ref[pl.ds(i, 1), :width], row)
        return row

    gate_s[...] = gate_of(pair, gate_s.shape[1])
    lent_gate[...] = gate_of(final, lent_gate.shape[1])
    ltm_s[...] = jnp.zeros_like(ltm_s)

    def visit(span, head, first, last, lent=False):
        base = q_heads if lent else head * group
        ok = mask_ref[final if lent else pair, span] > 0
        keys = kv[span, head, :, 0].reshape(2 * rows, HEAD_SIZE)
        vals = kv[span, head, :, 1].reshape(2 * rows, HEAD_SIZE)

        def held(ref):
            return ref[pl.ds(base, group)].reshape(tall, HEAD_SIZE)

        def keep(ref, value):
            ref[pl.ds(base, group)] = value.reshape(group, rows, HEAD_SIZE)

        score = factor * lax.dot_general(
            held(qbuf), keys, (((1,), (1,)), ((), ())),
            preferred_element_type=jnp.float32,
        )
        top = jnp.where(ok, jnp.max(score, axis=1, keepdims=True), -FAR)
        if not first:
            before = held(top_s)
            top = jnp.maximum(before, top)
        top = jnp.broadcast_to(top, (tall, HEAD_SIZE))
        less = jnp.where(ok, top, FAR)
        weights = [
            jnp.exp2(score[:, i:i + HEAD_SIZE] - less)
            for i in range(0, score.shape[1], HEAD_SIZE)
        ]
        total = functools.reduce(jnp.add, weights)
        weight = jnp.concatenate([w.astype(jnp.bfloat16) for w in weights], axis=1)
        acc = jnp.dot(weight, vals, preferred_element_type=jnp.float32)
        if not first:
            fade = jnp.exp2(before - top)
            total = total + held(tot_s) * fade
            acc = acc + held(acc_s) * fade
        if not last:
            keep(top_s, top)
            keep(tot_s, total)
            keep(acc_s, acc)
            return
        lane = lax.broadcasted_iota(jnp.int32, (rows, HEAD_SIZE), 1)
        sums = jnp.zeros_like(ltm_s) if lent else ltm_s[...]
        full = jnp.sum(total, axis=1, keepdims=True)
        attended = acc / full
        log_total = top * LN2 + jnp.log(full)
        for t in range(group):
            cut = slice(t * rows, (t + 1) * rows)
            if lent:
                cols = slice(t * HEAD_SIZE, (t + 1) * HEAD_SIZE)
                lent_out[t] = (lent_gate[:, cols] * attended[cut]).astype(lent_out.dtype)
                sums = jnp.where(lane == t, log_total[cut], sums)
            else:
                j = base + t
                cols = pl.ds(pl.multiple_of(j * HEAD_SIZE, HEAD_SIZE), HEAD_SIZE)
                out_ref[:, cols] = (gate_s[:, cols] * attended[cut]).astype(out_ref.dtype)
                sums = jnp.where(lane == j, log_total[cut], sums)
        if lent:
            lent_lt[...] = jnp.transpose(sums)[:lent_lt.shape[0]]
        else:
            ltm_s[...] = sums

    def loop(low, high, body):
        def step(i, carry):
            body(i)
            return carry

        lax.fori_loop(low, high, step, 0)

    @pl.when(at_bottom)
    def _():
        for h in range(far_from, kv_heads):
            arrive(pair, other, h)
            far_up(h).start()

        def all_heads(h):
            @pl.when(h < far_from)
            def _():
                arrive(pair, other, h)

            visit(pair, h, True, True)

        loop(0, kv_heads, all_heads)
        sent(up_sem.at[0], 0, kv_heads)
        sent(over_sem.at[0], 0, kv_heads)
        sent(up_sem.at[pairs], far_from, kv_heads)

    @pl.when(at_middle)
    def _():
        def pass_on(i):
            span = pair - i
            for h in heads:
                arrive(span, side, h)
                up(span, h)
                over(span, h)
                if h == 0:

                    @pl.when(i == 1)
                    def _():
                        own_up(0)

            @pl.when(span == 0)
            def _():
                for h in range(far_from, kv_heads):
                    arrive(0, other, h)
                    far_up(h).start()

        pass_on(1)

        def own_span(h):
            arrive(pair, other, h)
            visit(pair, h, True, False)

        loop(0, kv_heads, own_span)

        def further(i):
            pass_on(i)

            def between(h):
                arrive(pair - i + 1, other, h)
                visit(pair - i + 1, h, False, False)

            loop(0, kv_heads, between)

        loop(2, pair + 1, further)

        def ending(h):
            @pl.when(h < far_from)
            def _():
                arrive(0, other, h)

            visit(0, h, False, True)

        loop(0, kv_heads, ending)

        def settle(span):
            sent(up_sem.at[span], 0, kv_heads)
            sent(over_sem.at[span], 0, kv_heads)

        loop(1, pair + 1, settle)
        sent(up_sem.at[0], 0, kv_heads)
        sent(over_sem.at[0], 0, far_from)
        sent(up_sem.at[pairs], far_from, kv_heads)

    @pl.when(at_helper)
    def _():
        def own_span(h):
            arrive(pair, other, h)
            visit(pair, h, True, False)

        for h in range(1, kv_heads):
            arrive(pair - 1, side, h)
            up(pair - 1, h)
            if h == 1:
                arrive(final, side, 0)
                over(final, 0)
                for later in range(2, kv_heads):
                    own_over(later)
                own_span(0)
        own_span(1)
        lent_q().wait_recv()

        def further(i):
            span = pair - i
            arrive(span, side, 0)
            over(span, 0)

            @pl.when(i == 2)
            def _():
                visit(pair, 0, True, False, lent=True)
                arrive(final, other, 0)
                visit(final, 0, False, False, lent=True)
                for h in range(kv_heads):
                    if h == 0:
                        arrive(pair - 1, side, 0)
                    over(pair - 1, h)

            def rest(h):
                @pl.when((i == 2) & (h < top_head))
                def _():
                    own_span(h + 1)

                arrive(span, side, h)
                up(span, h)

                @pl.when(h == top_head - 1)
                def _():
                    arrive(span + 1, other, 0)
                    visit(span + 1, 0, False, False, lent=True)

            loop(1, kv_heads, rest)
            for h in range(1, kv_heads):
                over(span, h)

        loop(2, pair + 1, further)
        arrive(0, other, 0)
        visit(0, 0, False, True, lent=True)
        for j in range(group):
            give_back(j).start()
        give_totals().start()

        def remaining(i, last):
            span = pair - i

            def all_heads(h):
                @pl.when(h > 0)
                def _():
                    arrive(span, other, h)

                visit(span, h, False, last)

            loop(0, kv_heads, all_heads)

        loop(1, pair, lambda i: remaining(i, False))
        remaining(pair, True)

        def settle(span):
            sent(up_sem.at[span], 1, kv_heads)
            sent(over_sem.at[span], 0, kv_heads)

        loop(1, pair + 1, settle)
        sent(up_sem.at[0], 1, kv_heads)
        sent(over_sem.at[0], 0, far_from)
        sent(over_sem.at[final], 0, 1)
        given().wait_send()
        give_totals().wait_send()

    @pl.when(at_lender)
    def _():
        wide = kv_heads - 1

        def pass_on(n):
            span, h = pair - 1 - n // wide, 1 + n % wide
            arrive(span, side, h)
            move(span, side, h, over_sem.at[span], partner).start()

        def take(n, first, last):
            span, h = pair - n // wide, 1 + n % wide
            arrive(span, other, h)
            visit(span, h, first, last)

        def opening(n):
            pass_on(n)
            take(n, True, False)

        def between(n):
            pass_on(n)
            take(n, False, False)

        loop(0, wide, opening)
        loop(wide, wide * pair, between)
        loop(wide * pair, wide * (pair + 1), lambda n: take(n, False, True))

        sent(up_sem.at[pair], 0, 1)
        lent_q().wait_send()
        loop(0, pair + 1, lambda span: sent(over_sem.at[span], 1, kv_heads))
        given().wait_recv()
        give_totals().wait_recv()

    lt_ref[...] = jnp.transpose(ltm_s[...])[:q_heads]

    @pl.when(at_lender)
    def _():
        high = home_lt.shape[0]
        lt_ref[:high] = lt_ref[:high] + home_lt[...]


def finish(mixed_ref, log_ref, mixed_out, log_out, sem):
    parts = sem.shape[0] - 1
    high = mixed_ref.shape[0] // parts
    copies = [
        pltpu.make_async_copy(
            mixed_ref.at[pl.ds(i * high, high)],
            mixed_out.at[pl.ds(i * high, high)],
            sem.at[i],
        )
        for i in range(parts)
    ] + [pltpu.make_async_copy(log_ref, log_out, sem.at[parts])]
    for copy in copies:
        copy.start()
    for copy in copies:
        copy.wait()


def solution(mesh):
    count = mesh.shape["tm"]

    def on_device(queries, keys, values, span_mask, section, section_gate):
        rows = queries.shape[0]
        q_heads = queries.shape[1] // HEAD_SIZE
        kv_heads = keys.shape[1] // HEAD_SIZE
        group = q_heads // kv_heads
        assert CH == 2 * rows and count % 2 == 0 and count >= 8 and kv_heads > 2
        pairs = count // 2
        vmem = pl.BlockSpec(memory_space=pltpu.VMEM)
        dma = pltpu.SemaphoreType.DMA
        keep_near = lambda x: pltpu.with_memory_space_constraint(x, pltpu.VMEM)
        state = pltpu.VMEM((q_heads + group, rows, HEAD_SIZE), jnp.float32)
        held = pltpu.VMEM((pairs, kv_heads, 2, 2, rows, HEAD_SIZE), jnp.bfloat16)
        lent_lt = pltpu.VMEM((-(-group // 8) * 8, rows), jnp.float32)
        mixed, log_total = pl.pallas_call(
            functools.partial(kernel, pairs, kv_heads - 1),
            out_shape=(
                pltpu.VMEM(queries.shape, jnp.bfloat16),
                pltpu.VMEM((q_heads, rows), jnp.float32),
            ),
            in_specs=[pl.BlockSpec(memory_space=pltpu.HBM)] * 6,
            out_specs=(vmem, vmem),
            scratch_shapes=[
                pltpu.VMEM((q_heads + group, rows, HEAD_SIZE), jnp.bfloat16),
                held, state, state, state,
                pltpu.VMEM((rows, HEAD_SIZE), jnp.float32),
                pltpu.VMEM((1, queries.shape[1]), jnp.float32),
                pltpu.SMEM(span_mask.shape, jnp.int32),
                pltpu.SMEM(section.shape, jnp.int32),
                pltpu.VMEM(section_gate.shape, jnp.float32),
                pltpu.VMEM((group, rows, HEAD_SIZE), jnp.bfloat16),
                lent_lt,
                pltpu.VMEM((1, group * HEAD_SIZE), jnp.float32),
                lent_lt,
                dma((5,)), dma((count, kv_heads)), dma((pairs + 1,)), dma((pairs,)),
                dma((2,)), dma((4,)),
            ],
            compiler_params=pltpu.CompilerParams(
                collective_id=0, has_side_effects=True, vmem_limit_bytes=60*2**20
            ),
            name="span_attention",
        )(queries, keys, values, span_mask, section, section_gate)
        return pl.pallas_call(
            finish,
            out_shape=(
                jax.ShapeDtypeStruct(mixed.shape, mixed.dtype),
                jax.ShapeDtypeStruct(log_total.shape, log_total.dtype),
            ),
            in_specs=[vmem, vmem],
            out_specs=[pl.BlockSpec(memory_space=pltpu.HBM)] * 2,
            scratch_shapes=[dma((5,))],
            compiler_params=pltpu.CompilerParams(vmem_limit_bytes=4 * 2**20),
            name="write_back",
        )(keep_near(mixed), keep_near(log_total))

    placed = (
        P(("grp", "tm"), "head"),
        P(("grp", "tm"), "head"),
        P(("grp", "tm"), "head"),
        P("grp", None),
        P("grp"),
        P(None, "head"),
    )
    return jax.shard_map(
        on_device,
        mesh=mesh,
        in_specs=placed,
        out_specs=(P(("grp", "tm"), "head"), P("head", ("grp", "tm"))),
        check_vma=False,
    )
```

```python
import functools
import math

import jax
import jax.numpy as jnp
from jax import lax
from jax.experimental import pallas as pl
from jax.experimental.pallas import tpu as pltpu
from jax.sharding import PartitionSpec as P

HEAD_SIZE = 128
CH = 256
MESH = pl.DeviceIdType.MESH
LOG2E = 1.4426950408889634
LN2 = 0.6931471805599453
FAR = 1e30


def kernel(
    pairs, far_from, q_hbm, k_hbm, v_hbm, mask_hbm, sec_hbm, gate_hbm, out_ref, lt_ref,
    qbuf, kv, top_s, tot_s, acc_s, ltm_s, gate_s, mask_ref, sec_ref, gate_ref,
    lent_out, lent_lt, lent_gate, home_lt,
    local_sem, recv_sem, up_sem, over_sem, lend_sem, back_sem,
):
    rows = qbuf.shape[1]
    kv_heads = kv.shape[1]
    group = lent_out.shape[0]
    q_heads = kv_heads * group
    tall = group * rows
    final = pairs - 1
    top_head = kv_heads - 1
    factor = LOG2E / math.sqrt(HEAD_SIZE)

    me = lax.axis_index("tm")
    pair = me // 2
    side = me % 2
    other = 1 - side
    partner = me + 1 - 2 * side
    has_prev = pair > 0
    has_next = pair < final
    at_bottom = pair == 0
    at_lender = pair == final
    at_helper = pair == final - 1
    at_middle = has_prev & (pair < final - 1)

    barrier = pltpu.get_barrier_semaphore()

    def greet(when, target):
        @pl.when(when)
        def _():
            pl.semaphore_signal(barrier, inc=1, device_id={"tm": target}, device_id_type=MESH)

    greet(has_prev, me - 2)
    greet(at_helper, me + 2)
    pl.semaphore_signal(barrier, inc=1, device_id={"tm": partner}, device_id_type=MESH)
    pl.semaphore_wait(barrier, 1 + (has_next | at_lender).astype(jnp.int32))

    def copy_to(source, target_ref, send, receive, target):
        return pltpu.make_async_remote_copy(
            src_ref=source,
            dst_ref=target_ref,
            send_sem=send,
            recv_sem=receive,
            device_id={"tm": target},
            device_id_type=MESH,
        )

    def columns(ref, h):
        return ref.at[:, pl.ds(h * HEAD_SIZE, HEAD_SIZE)]

    def own(send, target, h):
        for i, source in enumerate((k_hbm, v_hbm)):
            copy_to(
                columns(source, h), kv.at[pair, h, side, i],
                send.at[pair], recv_sem.at[me, h, i], target,
            ).start()

    def own_up(h):
        own(up_sem, me + 2, h)

    def own_over(h):
        own(over_sem, partner, h)

    def move(span, edge, h, i, send, target):
        piece = kv.at[span, h, edge, i]
        return copy_to(piece, piece, send, recv_sem.at[2 * span + edge, h, i], target)

    def arrived(span, edge, h, i):
        move(span, edge, h, i, over_sem.at[span], partner).wait_recv()

    def arrive(span, edge, h):
        for i in range(2):
            arrived(span, edge, h, i)

    def up(span, h, i):
        move(span, side, h, i, up_sem.at[span], me + 2).start()

    def over(span, h, i):
        move(span, side, h, i, over_sem.at[span], partner).start()

    def over_if(span, h, i):
        if isinstance(h, int) and h < far_from:
            over(span, h, i)
        else:

            @pl.when((span > 0) | (h < far_from))
            def _():
                over(span, h, i)

    def both_over(span, h):
        for i in range(2):
            over_if(span, h, i)

    def relay(span, h, *ways):
        for i in range(2):
            arrived(span, side, h, i)
            for way in ways:
                way(span, h, i)

    def relay_far(h):
        for i in range(2):
            arrived(0, other, h, i)
            move(0, other, h, i, up_sem.at[pairs], me + 2).start()

    def sent(sem, low, high):
        some = kv.at[0, pl.ds(low, high - low), 0]
        copy_to(some, some, sem, recv_sem.at[0, 0, 0], partner).wait_send()

    def lend_q(j):
        return copy_to(columns(q_hbm, j), qbuf.at[q_heads + j], lend_sem.at[0], lend_sem.at[1], me - 2)

    def lent_q():
        whole = qbuf.at[pl.ds(q_heads, group)]
        return copy_to(whole, whole, lend_sem.at[0], lend_sem.at[1], me - 2)

    def give_back(j):
        return copy_to(lent_out.at[j], columns(out_ref, j), back_sem.at[0], back_sem.at[1], me + 2)

    def given():
        return copy_to(lent_out, lent_out, back_sem.at[0], back_sem.at[1], me + 2)

    def give_totals():
        return copy_to(lent_lt, home_lt, back_sem.at[2], back_sem.at[3], me + 2)

    heads = range(kv_heads)

    @pl.when(at_bottom)
    def _():
        for h in heads:
            own_up(h)
            own_over(h)

    @pl.when(at_middle)
    def _():
        for h in heads:
            if h > 0:
                own_up(h)
            own_over(h)

    @pl.when(at_helper)
    def _():
        for h in heads:
            if h > 0:
                own_up(h)
            if h < 2:
                own_over(h)

    @pl.when(at_lender)
    def _():
        own(up_sem, me - 2, 0)
        for h in heads:
            if h > 0:
                own_over(h)
        for j in range(group):
            lend_q(j).start()

    small = [
        pltpu.make_async_copy(mask_hbm, mask_ref, local_sem.at[0]),
        pltpu.make_async_copy(sec_hbm, sec_ref, local_sem.at[1]),
        pltpu.make_async_copy(gate_hbm, gate_ref, local_sem.at[2]),
    ]
    for copy in small:
        copy.start()
    for h in heads:
        for i, source in enumerate((k_hbm, v_hbm)):
            pltpu.make_async_copy(columns(source, h), kv.at[pair, h, side, i], local_sem.at[3]).start()
    for h in range(q_heads):
        pltpu.make_async_copy(columns(q_hbm, h), qbuf.at[h], local_sem.at[4]).start()
    for copy in small:
        copy.wait()
    mine = kv.at[pair, :, side]
    pltpu.make_async_copy(mine, mine, local_sem.at[3]).wait()
    mine = qbuf.at[pl.ds(0, q_heads)]
    pltpu.make_async_copy(mine, mine, local_sem.at[4]).wait()

    def gate_of(span, width):
        row = gate_ref[pl.ds(0, 1), :width]
        for i in range(1, gate_ref.shape[0]):
            row = jnp.where(sec_ref[span] == i, gate_ref[pl.ds(i, 1), :width], row)
        return row

    gate_s[...] = gate_of(pair, gate_s.shape[1])
    lent_gate[...] = gate_of(final, lent_gate.shape[1])
    ltm_s[...] = jnp.zeros_like(ltm_s)

    def visit(span, head, first, last, lent=False):
        base = q_heads if lent else head * group
        ok = mask_ref[final if lent else pair, span] > 0
        keys = kv[span, head, :, 0].reshape(2 * rows, HEAD_SIZE)
        vals = kv[span, head, :, 1].reshape(2 * rows, HEAD_SIZE)

        def held(ref):
            return ref[pl.ds(base, group)].reshape(tall, HEAD_SIZE)

        def keep(ref, value):
            ref[pl.ds(base, group)] = value.reshape(group, rows, HEAD_SIZE)

        score = factor * lax.dot_general(
            held(qbuf), keys, (((1,), (1,)), ((), ())),
            preferred_element_type=jnp.float32,
        )
        top = jnp.where(ok, jnp.max(score, axis=1, keepdims=True), -FAR)
        if not first:
            before = held(top_s)
            top = jnp.maximum(before, top)
        top = jnp.broadcast_to(top, (tall, HEAD_SIZE))
        less = jnp.where(ok, top, FAR)
        weights = [
            jnp.exp2(score[:, i:i + HEAD_SIZE] - less)
            for i in range(0, score.shape[1], HEAD_SIZE)
        ]
        total = functools.reduce(jnp.add, weights)
        weight = jnp.concatenate([w.astype(jnp.bfloat16) for w in weights], axis=1)
        acc = jnp.dot(weight, vals, preferred_element_type=jnp.float32)
        if not first:
            fade = jnp.exp2(before - top)
            total = total + held(tot_s) * fade
            acc = acc + held(acc_s) * fade
        if not last:
            keep(top_s, top)
            keep(tot_s, total)
            keep(acc_s, acc)
            return
        lane = lax.broadcasted_iota(jnp.int32, (rows, HEAD_SIZE), 1)
        sums = jnp.zeros_like(ltm_s) if lent else ltm_s[...]
        full = jnp.sum(total, axis=1, keepdims=True)
        attended = acc / full
        log_total = top * LN2 + jnp.log(full)
        for t in range(group):
            cut = slice(t * rows, (t + 1) * rows)
            if lent:
                cols = slice(t * HEAD_SIZE, (t + 1) * HEAD_SIZE)
                lent_out[t] = (lent_gate[:, cols] * attended[cut]).astype(lent_out.dtype)
                sums = jnp.where(lane == t, log_total[cut], sums)
            else:
                j = base + t
                cols = pl.ds(pl.multiple_of(j * HEAD_SIZE, HEAD_SIZE), HEAD_SIZE)
                out_ref[:, cols] = (gate_s[:, cols] * attended[cut]).astype(out_ref.dtype)
                sums = jnp.where(lane == j, log_total[cut], sums)
        if lent:
            lent_lt[...] = jnp.transpose(sums)[:lent_lt.shape[0]]
        else:
            ltm_s[...] = sums

    def loop(low, high, body):
        def step(i, carry):
            body(i)
            return carry

        lax.fori_loop(low, high, step, 0)

    @pl.when(at_bottom)
    def _():
        for h in range(far_from, kv_heads):
            relay_far(h)

        def all_heads(h):
            @pl.when(h < far_from)
            def _():
                arrive(pair, other, h)

            visit(pair, h, True, True)

        loop(0, kv_heads, all_heads)
        sent(up_sem.at[0], 0, kv_heads)
        sent(over_sem.at[0], 0, kv_heads)
        sent(up_sem.at[pairs], far_from, kv_heads)

    @pl.when(at_middle)
    def _():
        def pass_on(i):
            span = pair - i
            for h in heads:
                relay(span, h, up, over_if)
                if h == 0:

                    @pl.when(i == 1)
                    def _():
                        own_up(0)

            @pl.when(span == 0)
            def _():
                for h in range(far_from, kv_heads):
                    relay_far(h)

        pass_on(1)

        def own_span(h):
            arrive(pair, other, h)
            visit(pair, h, True, False)

        loop(0, kv_heads, own_span)

        def further(i):
            pass_on(i)

            def between(h):
                arrive(pair - i + 1, other, h)
                visit(pair - i + 1, h, False, False)

            loop(0, kv_heads, between)

        loop(2, pair + 1, further)

        def ending(h):
            @pl.when(h < far_from)
            def _():
                arrive(0, other, h)

            visit(0, h, False, True)

        loop(0, kv_heads, ending)

        def settle(span):
            sent(up_sem.at[span], 0, kv_heads)
            sent(over_sem.at[span], 0, kv_heads)

        loop(1, pair + 1, settle)
        sent(up_sem.at[0], 0, kv_heads)
        sent(over_sem.at[0], 0, far_from)
        sent(up_sem.at[pairs], far_from, kv_heads)

    @pl.when(at_helper)
    def _():
        def own_span(h):
            arrive(pair, other, h)
            visit(pair, h, True, False)

        for h in range(1, kv_heads):
            relay(pair - 1, h, up)
            if h == 1:
                relay(final, 0, over)
                for later in range(2, kv_heads):
                    own_over(later)
                own_span(0)
        own_span(1)
        lent_q().wait_recv()

        def further(i):
            span = pair - i
            relay(span, 0, over)

            @pl.when(i == 2)
            def _():
                visit(pair, 0, True, False, lent=True)
                arrive(final, other, 0)
                visit(final, 0, False, False, lent=True)
                relay(pair - 1, 0, over)
                for h in range(1, kv_heads):
                    both_over(pair - 1, h)

            def rest(h):
                @pl.when((i == 2) & (h < top_head))
                def _():
                    own_span(h + 1)

                relay(span, h, up)

                @pl.when(h == top_head)
                def _():
                    arrive(span + 1, other, 0)
                    visit(span + 1, 0, False, False, lent=True)

            loop(1, kv_heads, rest)
            for h in range(1, kv_heads):
                both_over(span, h)

        loop(2, pair + 1, further)
        arrive(0, other, 0)
        visit(0, 0, False, True, lent=True)
        for j in range(group):
            give_back(j).start()
        give_totals().start()

        def remaining(i, last):
            span = pair - i

            def all_heads(h):
                @pl.when(h > 0)
                def _():
                    arrive(span, other, h)

                visit(span, h, False, last)

            loop(0, kv_heads, all_heads)

        loop(1, pair, lambda i: remaining(i, False))
        remaining(pair, True)

        def settle(span):
            sent(up_sem.at[span], 1, kv_heads)
            sent(over_sem.at[span], 0, kv_heads)

        loop(1, pair + 1, settle)
        sent(up_sem.at[0], 1, kv_heads)
        sent(over_sem.at[0], 0, far_from)
        sent(over_sem.at[final], 0, 1)
        given().wait_send()
        give_totals().wait_send()

    @pl.when(at_lender)
    def _():
        wide = kv_heads - 1

        def pass_on(n):
            span, h = pair - 1 - n // wide, 1 + n % wide
            relay(span, h, over)

        def take(n, first, last):
            span, h = pair - n // wide, 1 + n % wide
            arrive(span, other, h)
            visit(span, h, first, last)

        def opening(n):
            pass_on(n)
            take(n, True, False)

        def between(n):
            pass_on(n)
            take(n, False, False)

        loop(0, wide, opening)
        loop(wide, wide * pair, between)
        loop(wide * pair, wide * (pair + 1), lambda n: take(n, False, True))

        sent(up_sem.at[pair], 0, 1)
        lent_q().wait_send()
        loop(0, pair + 1, lambda span: sent(over_sem.at[span], 1, kv_heads))
        given().wait_recv()
        give_totals().wait_recv()

    lt_ref[...] = jnp.transpose(ltm_s[...])[:q_heads]

    @pl.when(at_lender)
    def _():
        high = home_lt.shape[0]
        lt_ref[:high] = lt_ref[:high] + home_lt[...]


def finish(mixed_ref, log_ref, mixed_out, log_out, sem):
    parts = sem.shape[0] - 1
    high = mixed_ref.shape[0] // parts
    copies = [
        pltpu.make_async_copy(
            mixed_ref.at[pl.ds(i * high, high)],
            mixed_out.at[pl.ds(i * high, high)],
            sem.at[i],
        )
        for i in range(parts)
    ] + [pltpu.make_async_copy(log_ref, log_out, sem.at[parts])]
    for copy in copies:
        copy.start()
    for copy in copies:
        copy.wait()


def solution(mesh):
    count = mesh.shape["tm"]

    def on_device(queries, keys, values, span_mask, section, section_gate):
        rows = queries.shape[0]
        q_heads = queries.shape[1] // HEAD_SIZE
        kv_heads = keys.shape[1] // HEAD_SIZE
        group = q_heads // kv_heads
        assert CH == 2 * rows and count % 2 == 0 and count >= 8 and kv_heads > 2
        pairs = count // 2
        vmem = pl.BlockSpec(memory_space=pltpu.VMEM)
        dma = pltpu.SemaphoreType.DMA
        keep_near = lambda x: pltpu.with_memory_space_constraint(x, pltpu.VMEM)
        state = pltpu.VMEM((q_heads + group, rows, HEAD_SIZE), jnp.float32)
        held = pltpu.VMEM((pairs, kv_heads, 2, 2, rows, HEAD_SIZE), jnp.bfloat16)
        lent_lt = pltpu.VMEM((-(-group // 8) * 8, rows), jnp.float32)
        mixed, log_total = pl.pallas_call(
            functools.partial(kernel, pairs, kv_heads - 2),
            out_shape=(
                pltpu.VMEM(queries.shape, jnp.bfloat16),
                pltpu.VMEM((q_heads, rows), jnp.float32),
            ),
            in_specs=[pl.BlockSpec(memory_space=pltpu.HBM)] * 6,
            out_specs=(vmem, vmem),
            scratch_shapes=[
                pltpu.VMEM((q_heads + group, rows, HEAD_SIZE), jnp.bfloat16),
                held, state, state, state,
                pltpu.VMEM((rows, HEAD_SIZE), jnp.float32),
                pltpu.VMEM((1, queries.shape[1]), jnp.float32),
                pltpu.SMEM(span_mask.shape, jnp.int32),
                pltpu.SMEM(section.shape, jnp.int32),
                pltpu.VMEM(section_gate.shape, jnp.float32),
                pltpu.VMEM((group, rows, HEAD_SIZE), jnp.bfloat16),
                lent_lt,
                pltpu.VMEM((1, group * HEAD_SIZE), jnp.float32),
                lent_lt,
                dma((5,)), dma((count, kv_heads, 2)), dma((pairs + 1,)), dma((pairs,)),
                dma((2,)), dma((4,)),
            ],
            compiler_params=pltpu.CompilerParams(
                collective_id=0, has_side_effects=True, vmem_limit_bytes=60*2**20
            ),
            name="span_attention",
        )(queries, keys, values, span_mask, section, section_gate)
        return pl.pallas_call(
            finish,
            out_shape=(
                jax.ShapeDtypeStruct(mixed.shape, mixed.dtype),
                jax.ShapeDtypeStruct(log_total.shape, log_total.dtype),
            ),
            in_specs=[vmem, vmem],
            out_specs=[pl.BlockSpec(memory_space=pltpu.HBM)] * 2,
            scratch_shapes=[dma((5,))],
            compiler_params=pltpu.CompilerParams(vmem_limit_bytes=4 * 2**20),
            name="write_back",
        )(keep_near(mixed), keep_near(log_total))

    placed = (
        P(("grp", "tm"), "head"),
        P(("grp", "tm"), "head"),
        P(("grp", "tm"), "head"),
        P("grp", None),
        P("grp"),
        P(None, "head"),
    )
    return jax.shard_map(
        on_device,
        mesh=mesh,
        in_specs=placed,
        out_specs=(P(("grp", "tm"), "head"), P("head", ("grp", "tm"))),
        check_vma=False,
    )
```

```python
import functools
import math

import jax
import jax.numpy as jnp
from jax import lax
from jax.experimental import pallas as pl
from jax.experimental.pallas import tpu as pltpu
from jax.sharding import PartitionSpec as P

HEAD_SIZE = 128
CH = 256
MESH = pl.DeviceIdType.MESH
LOG2E = 1.4426950408889634
LN2 = 0.6931471805599453
FAR = 1e30


def kernel(
    pairs, far_from, q_hbm, k_hbm, v_hbm, mask_hbm, sec_hbm, gate_hbm, out_ref, lt_ref,
    qbuf, kv, top_s, tot_s, acc_s, ltm_s, gate_s, mask_ref, sec_ref, gate_ref,
    lent_out, lent_lt, lent_gate, home_lt,
    local_sem, recv_sem, up_sem, over_sem, lend_sem, back_sem,
):
    rows = qbuf.shape[1]
    kv_heads = kv.shape[1]
    group = lent_out.shape[0]
    q_heads = kv_heads * group
    tall = group * rows
    final = pairs - 1
    top_head = kv_heads - 1
    factor = LOG2E / math.sqrt(HEAD_SIZE)

    me = lax.axis_index("tm")
    pair = me // 2
    side = me % 2
    other = 1 - side
    partner = me + 1 - 2 * side
    has_prev = pair > 0
    has_next = pair < final
    at_bottom = pair == 0
    at_lender = pair == final
    at_helper = pair == final - 1
    at_middle = has_prev & (pair < final - 1)

    barrier = pltpu.get_barrier_semaphore()

    def greet(when, target):
        @pl.when(when)
        def _():
            pl.semaphore_signal(barrier, inc=1, device_id={"tm": target}, device_id_type=MESH)

    greet(has_prev, me - 2)
    greet(at_helper, me + 2)
    pl.semaphore_signal(barrier, inc=1, device_id={"tm": partner}, device_id_type=MESH)
    heads = range(kv_heads)

    def columns(ref, h):
        return ref.at[:, pl.ds(h * HEAD_SIZE, HEAD_SIZE)]

    small = [
        pltpu.make_async_copy(mask_hbm, mask_ref, local_sem.at[0]),
        pltpu.make_async_copy(sec_hbm, sec_ref, local_sem.at[1]),
        pltpu.make_async_copy(gate_hbm, gate_ref, local_sem.at[2]),
    ]
    for copy in small:
        copy.start()
    for h in heads:
        for i, source in enumerate((k_hbm, v_hbm)):
            pltpu.make_async_copy(columns(source, h), kv.at[pair, h, side, i], local_sem.at[3]).start()
    for h in range(q_heads):
        pltpu.make_async_copy(columns(q_hbm, h), qbuf.at[h], local_sem.at[4]).start()

    pl.semaphore_wait(barrier, 1 + (has_next | at_lender).astype(jnp.int32))

    def copy_to(source, target_ref, send, receive, target):
        return pltpu.make_async_remote_copy(
            src_ref=source,
            dst_ref=target_ref,
            send_sem=send,
            recv_sem=receive,
            device_id={"tm": target},
            device_id_type=MESH,
        )

    def own(send, target, h):
        for i, source in enumerate((k_hbm, v_hbm)):
            copy_to(
                columns(source, h), kv.at[pair, h, side, i],
                send.at[pair], recv_sem.at[me, h, i], target,
            ).start()

    def own_up(h):
        own(up_sem, me + 2, h)

    def own_over(h):
        own(over_sem, partner, h)

    def move(span, edge, h, i, send, target):
        piece = kv.at[span, h, edge, i]
        return copy_to(piece, piece, send, recv_sem.at[2 * span + edge, h, i], target)

    def arrived(span, edge, h, i):
        move(span, edge, h, i, over_sem.at[span], partner).wait_recv()

    def arrive(span, edge, h):
        for i in range(2):
            arrived(span, edge, h, i)

    def up(span, h, i):
        move(span, side, h, i, up_sem.at[span], me + 2).start()

    def over(span, h, i):
        move(span, side, h, i, over_sem.at[span], partner).start()

    def over_if(span, h, i):
        if isinstance(h, int) and h < far_from:
            over(span, h, i)
        else:

            @pl.when((span > 0) | (h < far_from))
            def _():
                over(span, h, i)

    def both_over(span, h):
        for i in range(2):
            over_if(span, h, i)

    def relay(span, h, *ways):
        for i in range(2):
            arrived(span, side, h, i)
            for way in ways:
                way(span, h, i)

    def relay_far(h):
        for i in range(2):
            arrived(0, other, h, i)
            move(0, other, h, i, up_sem.at[pairs], me + 2).start()

    def sent(sem, low, high):
        some = kv.at[0, pl.ds(low, high - low), 0]
        copy_to(some, some, sem, recv_sem.at[0, 0, 0], partner).wait_send()

    def lend_q(j):
        return copy_to(columns(q_hbm, j), qbuf.at[q_heads + j], lend_sem.at[0], lend_sem.at[1], me - 2)

    def lent_q():
        whole = qbuf.at[pl.ds(q_heads, group)]
        return copy_to(whole, whole, lend_sem.at[0], lend_sem.at[1], me - 2)

    def give_back(j):
        return copy_to(lent_out.at[j], columns(out_ref, j), back_sem.at[0], back_sem.at[1], me + 2)

    def given():
        return copy_to(lent_out, lent_out, back_sem.at[0], back_sem.at[1], me + 2)

    def give_totals():
        return copy_to(lent_lt, home_lt, back_sem.at[2], back_sem.at[3], me + 2)

    @pl.when(at_bottom)
    def _():
        for h in heads:
            own_up(h)
            own_over(h)

    @pl.when(at_middle)
    def _():
        for h in heads:
            if h > 0:
                own_up(h)
            own_over(h)

    @pl.when(at_helper)
    def _():
        for h in heads:
            if h > 0:
                own_up(h)
            if h < 2:
                own_over(h)

    @pl.when(at_lender)
    def _():
        own(up_sem, me - 2, 0)
        for h in heads:
            if h > 0:
                own_over(h)
        for j in range(group):
            lend_q(j).start()

    for copy in small:
        copy.wait()
    mine = kv.at[pair, :, side]
    pltpu.make_async_copy(mine, mine, local_sem.at[3]).wait()
    mine = qbuf.at[pl.ds(0, q_heads)]
    pltpu.make_async_copy(mine, mine, local_sem.at[4]).wait()

    def gate_of(span, width):
        row = gate_ref[pl.ds(0, 1), :width]
        for i in range(1, gate_ref.shape[0]):
            row = jnp.where(sec_ref[span] == i, gate_ref[pl.ds(i, 1), :width], row)
        return row

    gate_s[...] = gate_of(pair, gate_s.shape[1])
    lent_gate[...] = gate_of(final, lent_gate.shape[1])
    ltm_s[...] = jnp.zeros_like(ltm_s)

    def visit(span, head, first, last, lent=False):
        base = q_heads if lent else head * group
        ok = mask_ref[final if lent else pair, span] > 0
        keys = kv[span, head, :, 0].reshape(2 * rows, HEAD_SIZE)
        vals = kv[span, head, :, 1].reshape(2 * rows, HEAD_SIZE)

        def held(ref):
            return ref[pl.ds(base, group)].reshape(tall, HEAD_SIZE)

        def keep(ref, value):
            ref[pl.ds(base, group)] = value.reshape(group, rows, HEAD_SIZE)

        score = factor * lax.dot_general(
            held(qbuf), keys, (((1,), (1,)), ((), ())),
            preferred_element_type=jnp.float32,
        )
        top = jnp.where(ok, jnp.max(score, axis=1, keepdims=True), -FAR)
        if not first:
            before = held(top_s)
            top = jnp.maximum(before, top)
        top = jnp.broadcast_to(top, (tall, HEAD_SIZE))
        less = jnp.where(ok, top, FAR)
        weights = [
            jnp.exp2(score[:, i:i + HEAD_SIZE] - less)
            for i in range(0, score.shape[1], HEAD_SIZE)
        ]
        total = functools.reduce(jnp.add, weights)
        weight = jnp.concatenate([w.astype(jnp.bfloat16) for w in weights], axis=1)
        acc = jnp.dot(weight, vals, preferred_element_type=jnp.float32)
        if not first:
            fade = jnp.exp2(before - top)
            total = total + held(tot_s) * fade
            acc = acc + held(acc_s) * fade
        if not last:
            keep(top_s, top)
            keep(tot_s, total)
            keep(acc_s, acc)
            return
        lane = lax.broadcasted_iota(jnp.int32, (rows, HEAD_SIZE), 1)
        sums = jnp.zeros_like(ltm_s) if lent else ltm_s[...]
        full = jnp.sum(total, axis=1, keepdims=True)
        attended = acc / full
        log_total = top * LN2 + jnp.log(full)
        for t in range(group):
            cut = slice(t * rows, (t + 1) * rows)
            if lent:
                cols = slice(t * HEAD_SIZE, (t + 1) * HEAD_SIZE)
                lent_out[t] = (lent_gate[:, cols] * attended[cut]).astype(lent_out.dtype)
                sums = jnp.where(lane == t, log_total[cut], sums)
            else:
                j = base + t
                cols = pl.ds(pl.multiple_of(j * HEAD_SIZE, HEAD_SIZE), HEAD_SIZE)
                out_ref[:, cols] = (gate_s[:, cols] * attended[cut]).astype(out_ref.dtype)
                sums = jnp.where(lane == j, log_total[cut], sums)
        if lent:
            lent_lt[...] = jnp.transpose(sums)[:lent_lt.shape[0]]
        else:
            ltm_s[...] = sums

    def loop(low, high, body):
        def step(i, carry):
            body(i)
            return carry

        lax.fori_loop(low, high, step, 0)

    @pl.when(at_bottom)
    def _():
        for h in range(far_from, kv_heads):
            relay_far(h)

        def all_heads(h):
            @pl.when(h < far_from)
            def _():
                arrive(pair, other, h)

            visit(pair, h, True, True)

        loop(0, kv_heads, all_heads)
        sent(up_sem.at[0], 0, kv_heads)
        sent(over_sem.at[0], 0, kv_heads)
        sent(up_sem.at[pairs], far_from, kv_heads)

    @pl.when(at_middle)
    def _():
        def pass_on(i):
            span = pair - i
            for h in heads:
                relay(span, h, up, over_if)
                if h == 0:

                    @pl.when(i == 1)
                    def _():
                        own_up(0)

            @pl.when(span == 0)
            def _():
                for h in range(far_from, kv_heads):
                    relay_far(h)

        pass_on(1)

        def own_span(h):
            arrive(pair, other, h)
            visit(pair, h, True, False)

        loop(0, kv_heads, own_span)

        def further(i):
            pass_on(i)

            def between(h):
                arrive(pair - i + 1, other, h)
                visit(pair - i + 1, h, False, False)

            loop(0, kv_heads, between)

        loop(2, pair + 1, further)

        def ending(h):
            @pl.when(h < far_from)
            def _():
                arrive(0, other, h)

            visit(0, h, False, True)

        loop(0, kv_heads, ending)

        def settle(span):
            sent(up_sem.at[span], 0, kv_heads)
            sent(over_sem.at[span], 0, kv_heads)

        loop(1, pair + 1, settle)
        sent(up_sem.at[0], 0, kv_heads)
        sent(over_sem.at[0], 0, far_from)
        sent(up_sem.at[pairs], far_from, kv_heads)

    @pl.when(at_helper)
    def _():
        def own_span(h):
            arrive(pair, other, h)
            visit(pair, h, True, False)

        for h in range(1, kv_heads):
            relay(pair - 1, h, up)
            if h == 1:
                relay(final, 0, over)
                for later in range(2, kv_heads):
                    own_over(later)
                own_span(0)
        own_span(1)
        lent_q().wait_recv()

        def further(i):
            span = pair - i
            relay(span, 0, over)

            @pl.when(i == 2)
            def _():
                visit(pair, 0, True, False, lent=True)
                arrive(final, other, 0)
                visit(final, 0, False, False, lent=True)
                relay(pair - 1, 0, over)
                for h in range(1, kv_heads):
                    both_over(pair - 1, h)

            def rest(h):
                @pl.when((i == 2) & (h < top_head))
                def _():
                    own_span(h + 1)

                relay(span, h, up)

                @pl.when(h == top_head)
                def _():
                    arrive(span + 1, other, 0)
                    visit(span + 1, 0, False, False, lent=True)

            loop(1, kv_heads, rest)
            for h in range(1, kv_heads):
                both_over(span, h)

        loop(2, pair + 1, further)
        arrive(0, other, 0)
        visit(0, 0, False, True, lent=True)
        for j in range(group):
            give_back(j).start()
        give_totals().start()

        def remaining(i, last):
            span = pair - i

            def all_heads(h):
                @pl.when(h > 0)
                def _():
                    arrive(span, other, h)

                visit(span, h, False, last)

            loop(0, kv_heads, all_heads)

        loop(1, pair, lambda i: remaining(i, False))
        remaining(pair, True)

        def settle(span):
            sent(up_sem.at[span], 1, kv_heads)
            sent(over_sem.at[span], 0, kv_heads)

        loop(1, pair + 1, settle)
        sent(up_sem.at[0], 1, kv_heads)
        sent(over_sem.at[0], 0, far_from)
        sent(over_sem.at[final], 0, 1)
        given().wait_send()
        give_totals().wait_send()

    @pl.when(at_lender)
    def _():
        wide = kv_heads - 1

        def pass_on(n):
            span, h = pair - 1 - n // wide, 1 + n % wide
            relay(span, h, over)

        def take(n, first, last):
            span, h = pair - n // wide, 1 + n % wide
            arrive(span, other, h)
            visit(span, h, first, last)

        def opening(n):
            pass_on(n)
            take(n, True, False)

        def between(n):
            pass_on(n)
            take(n, False, False)

        loop(0, wide, opening)
        loop(wide, wide * pair, between)
        loop(wide * pair, wide * (pair + 1), lambda n: take(n, False, True))

        sent(up_sem.at[pair], 0, 1)
        lent_q().wait_send()
        loop(0, pair + 1, lambda span: sent(over_sem.at[span], 1, kv_heads))
        given().wait_recv()
        give_totals().wait_recv()

    lt_ref[...] = jnp.transpose(ltm_s[...])[:q_heads]

    @pl.when(at_lender)
    def _():
        high = home_lt.shape[0]
        lt_ref[:high] = lt_ref[:high] + home_lt[...]


def finish(mixed_ref, log_ref, mixed_out, log_out, sem):
    parts = sem.shape[0] - 1
    high = mixed_ref.shape[0] // parts
    copies = [
        pltpu.make_async_copy(
            mixed_ref.at[pl.ds(i * high, high)],
            mixed_out.at[pl.ds(i * high, high)],
            sem.at[i],
        )
        for i in range(parts)
    ] + [pltpu.make_async_copy(log_ref, log_out, sem.at[parts])]
    for copy in copies:
        copy.start()
    for copy in copies:
        copy.wait()


def solution(mesh):
    count = mesh.shape["tm"]

    def on_device(queries, keys, values, span_mask, section, section_gate):
        rows = queries.shape[0]
        q_heads = queries.shape[1] // HEAD_SIZE
        kv_heads = keys.shape[1] // HEAD_SIZE
        group = q_heads // kv_heads
        assert CH == 2 * rows and count % 2 == 0 and count >= 8 and kv_heads > 2
        pairs = count // 2
        vmem = pl.BlockSpec(memory_space=pltpu.VMEM)
        dma = pltpu.SemaphoreType.DMA
        keep_near = lambda x: pltpu.with_memory_space_constraint(x, pltpu.VMEM)
        state = pltpu.VMEM((q_heads + group, rows, HEAD_SIZE), jnp.float32)
        held = pltpu.VMEM((pairs, kv_heads, 2, 2, rows, HEAD_SIZE), jnp.bfloat16)
        lent_lt = pltpu.VMEM((-(-group // 8) * 8, rows), jnp.float32)
        mixed, log_total = pl.pallas_call(
            functools.partial(kernel, pairs, kv_heads - 2),
            out_shape=(
                pltpu.VMEM(queries.shape, jnp.bfloat16),
                pltpu.VMEM((q_heads, rows), jnp.float32),
            ),
            in_specs=[pl.BlockSpec(memory_space=pltpu.HBM)] * 6,
            out_specs=(vmem, vmem),
            scratch_shapes=[
                pltpu.VMEM((q_heads + group, rows, HEAD_SIZE), jnp.bfloat16),
                held, state, state, state,
                pltpu.VMEM((rows, HEAD_SIZE), jnp.float32),
                pltpu.VMEM((1, queries.shape[1]), jnp.float32),
                pltpu.SMEM(span_mask.shape, jnp.int32),
                pltpu.SMEM(section.shape, jnp.int32),
                pltpu.VMEM(section_gate.shape, jnp.float32),
                pltpu.VMEM((group, rows, HEAD_SIZE), jnp.bfloat16),
                lent_lt,
                pltpu.VMEM((1, group * HEAD_SIZE), jnp.float32),
                lent_lt,
                dma((5,)), dma((count, kv_heads, 2)), dma((pairs + 1,)), dma((pairs,)),
                dma((2,)), dma((4,)),
            ],
            compiler_params=pltpu.CompilerParams(
                collective_id=0, has_side_effects=True, vmem_limit_bytes=60*2**20
            ),
            name="span_attention",
        )(queries, keys, values, span_mask, section, section_gate)
        return pl.pallas_call(
            finish,
            out_shape=(
                jax.ShapeDtypeStruct(mixed.shape, mixed.dtype),
                jax.ShapeDtypeStruct(log_total.shape, log_total.dtype),
            ),
            in_specs=[vmem, vmem],
            out_specs=[pl.BlockSpec(memory_space=pltpu.HBM)] * 2,
            scratch_shapes=[dma((5,))],
            compiler_params=pltpu.CompilerParams(vmem_limit_bytes=4 * 2**20),
            name="write_back",
        )(keep_near(mixed), keep_near(log_total))

    placed = (
        P(("grp", "tm"), "head"),
        P(("grp", "tm"), "head"),
        P(("grp", "tm"), "head"),
        P("grp", None),
        P("grp"),
        P(None, "head"),
    )
    return jax.shard_map(
        on_device,
        mesh=mesh,
        in_specs=placed,
        out_specs=(P(("grp", "tm"), "head"), P("head", ("grp", "tm"))),
        check_vma=False,
    )
```
